32 devices in a mesh: groups: 2 (over y), dp: 4 (over z), rep: 4 (over x, core).
Axes of the slice: x: 2, y: 2, z: 4, core: 2. Of those that a mesh axis runs over, the one named last changes fastest.
Arguments:
- latent_store: bfloat16 [8, 48, 576, 128], P(('groups', 'dp'), 'rep'), parts along dimension 0, may hold values from -6 to 6
- page_rank: int32 [8, 48], P('groups', 'rep'), parts along dimension 0, may hold values from 0 to 3, as said below
- page_index: int32 [8, 48], P('groups', 'rep'), parts along dimension 0, may hold values from 0 to 11, as said below
- lengths: int32 [8, 1], P('groups'), parts along dimension 0, may hold values from 1536 to 6144, as said below
- queries: bfloat16 [16, 36864], P(('groups', 'dp')), parts along dimension 0, may hold values from -250 to 250
- new_latent: bfloat16 [16, 576], P(('groups', 'dp')), parts along dimension 0, may hold values from -4 to 4
- up_value: bfloat16 [64, 512, 128], P('dp'), may hold values from -0.25 to 0.25
- out_proj: bfloat16 [8192, 7168], P('dp', 'rep'), may hold values from -0.0625 to 0.0625
- residual: bfloat16 [16, 7168], P(('groups', 'dp'), 'rep'), parts along dimension 0, may hold values from -11 to 11
- norm_gain: float32 [7168], P('rep'), may hold values from 0.1 to 1.9
- w_gate: bfloat16 [7168, 12288], P('rep', 'dp'), may hold values from -0.0625 to 0.0625
- w_up: bfloat16 [7168, 12288], P('rep', 'dp'), may hold values from -0.0625 to 0.0625
- w_down: bfloat16 [12288, 7168], P('dp', 'rep'), may hold values from -0.0546875 to 0.0546875
Outputs:
- layer_out: bfloat16 [16, 7168], P(('groups', 'dp'), 'rep'), parts along dimension 0
The draws below stay inside these ranges and needn't reach their ends.
There are 2 independent parts, one for each index of `groups`. The reference program is written for one: setup_inputs(seed, part) draws one part's arguments, and reference() takes and returns one part's arrays. A program takes and returns all parts, laid end to end along the dimension named above; an argument that names none is the same for every part. Nothing has to cross between parts.
Inputs may be any that keep to these rules, and one draw needn't show every extreme that they name: page_rank[d, q] is the storage rank holding slot q of rank d, on its device with rep index q // 12; one storage device holds at most 3 slot of one rank, and some holds exactly 3. page_index[d, q] is the slot's page among the 12 pages of its storage device; over all ranks every page of every storage device is named by exactly one slot. `lengths`: some request has exactly 6144 tokens.
All inputs are finite; a program needn't handle non-finite values.
Results may differ from the reference program's by a relative error of at most 0.015.
Values may be sent and summed in bfloat16 or wider, within the bound.
No kernel may reach another device: no remote copies, remote signals or barrier semaphores. Data moves between devices by JAX's collectives and lax.ppermute only.
A program may use at most 128 MiB of HBM per device.

```python
import jax
import jax.numpy as jnp
from jax import lax

D = 7168
HEADS = 64
CKV = 512
ROPE = 64
VDIM = 128
FF = 12288
PAGE = 128
STEPS = 2
REQ_DP = 1
PAGES = 48
LAT = 576
ROWS = 8
RANKS = 4
QSLOTS = 48
SLOT_DEV = 12


def permute_rows(source_key, count, length):
    row_keys = jax.random.split(source_key, count)
    return jax.vmap(lambda single: jax.random.permutation(single, length))(row_keys).astype(jnp.int32)


def page_tables(key):
    base_key = jax.random.fold_in(key, 11)
    columns = QSLOTS // SLOT_DEV
    key_list = jax.random.split(base_key, 5)
    outer_perm = permute_rows(key_list[0], columns, RANKS)
    inner_perm = permute_rows(key_list[1], columns, RANKS)
    offset_perm = permute_rows(key_list[2], columns, RANKS)
    virtual_slot = permute_rows(key_list[3], columns * RANKS, SLOT_DEV).reshape(columns, RANKS, SLOT_DEV)
    store_perm = permute_rows(key_list[4], columns * RANKS, SLOT_DEV).reshape(columns, RANKS * SLOT_DEV)
    offset_table = jnp.broadcast_to(offset_perm[:, None, :], (columns, RANKS, RANKS))
    offsets = jnp.take_along_axis(offset_table, virtual_slot % RANKS, axis=2)
    position = (inner_perm[:, :, None] + offsets) % RANKS
    outer_table = jnp.broadcast_to(outer_perm[:, None, :], (columns, RANKS, RANKS))
    source_rank = jnp.take_along_axis(outer_table, position, axis=2)
    store_table = jnp.broadcast_to(store_perm[:, None, :], (columns, RANKS, RANKS * SLOT_DEV))
    store_slot = jnp.take_along_axis(store_table, source_rank * SLOT_DEV + virtual_slot, axis=2)
    rank_table = source_rank.transpose(1, 0, 2).reshape(RANKS, QSLOTS).astype(jnp.int32)
    index_table = store_slot.transpose(1, 0, 2).reshape(RANKS, QSLOTS).astype(jnp.int32)
    return (rank_table, index_table)


def draw_page_rank(key, part):
    return page_tables(key)[0]


def draw_page_index(key, part):
    return page_tables(key)[1]


def draw_lengths(key, part):
    base_key = jax.random.fold_in(key, 31)
    first_key, second_key = jax.random.split(base_key)
    longest = PAGES * PAGE
    drawn = jax.random.randint(first_key, (RANKS * REQ_DP,), longest // 4, longest + 1, dtype=jnp.int32)
    marked = jax.random.randint(second_key, (), 0, RANKS * REQ_DP, dtype=jnp.int32)
    drawn = drawn.at[marked].set(longest)
    return drawn.reshape(RANKS, REQ_DP).astype(jnp.int32)


def latent_rows(key):
    base_key = jax.random.fold_in(key, 47)
    fresh = jax.random.truncated_normal(base_key, -4.0, 4.0, (ROWS // STEPS, STEPS, LAT), jnp.float32)
    return fresh


def draw_new_latent(key, part):
    return latent_rows(key).reshape(ROWS, LAT).astype(jnp.bfloat16)


def draw_queries(key, part):
    fresh = latent_rows(key)
    base_key = jax.random.fold_in(key, 53)
    first_key = jax.random.fold_in(base_key, 0)
    drawn = jax.random.truncated_normal(first_key, -4.0, 4.0, (ROWS // STEPS, STEPS, HEADS, LAT), jnp.float32)
    target = jnp.broadcast_to(fresh[:, :, None, CKV:], (ROWS // STEPS, STEPS, HEADS, ROPE))
    strength = jnp.full((ROWS // STEPS, STEPS, HEADS), 1.6, jnp.float32)
    drawn = drawn.at[..., CKV:].add(strength[..., None] * target)
    return drawn.reshape(ROWS, HEADS * LAT).astype(jnp.bfloat16)


def draw_residual(key, part):
    base_key = jax.random.fold_in(key, 61)
    first_key = jax.random.fold_in(base_key, 0)
    column = jnp.arange(D, dtype=jnp.float32) / D
    values = jax.random.truncated_normal(first_key, -5.0, 5.0, (ROWS, D), jnp.float32) * (1.0 + 0.8 * column)
    return values.astype(jnp.bfloat16)


def shard_levels(stream_key, shape, cuts, smallest, largest):
    gain, own = 1.0, jax.random.fold_in(stream_key, 6)
    for dim, shards_of in cuts:
        steps = jnp.exp(jax.random.uniform(jax.random.fold_in(own, dim), (shards_of,), jnp.float32, smallest / len(cuts), largest / len(cuts)))
        gain = gain * jnp.repeat(steps, shape[dim] // shards_of).reshape([-1 if axis == dim else 1 for axis in range(len(shape))])
    return gain


def gaussian(key, shape, width, bound, pieces=(), kind=jnp.bfloat16):
    result = jax.random.normal(key, shape, jnp.float32) * width
    if len(pieces) > 0:
        result = shard_levels(key, shape, pieces, -0.22, 0.18) * result
    return jnp.clip(result, min=-bound, max=bound).astype(kind)


def setup_inputs(seed: int = 0, part: int = 0) -> dict:
    seeds = jax.random.split(jax.random.key(seed), 14)
    part_splits = jax.random.split(jax.random.fold_in(seeds[13], part), 14)
    latent_store = gaussian(part_splits[0], (RANKS, QSLOTS, LAT, PAGE), 1.0, 6.0, ((0, 4), (1, 4)))
    page_rank = draw_page_rank(jax.random.fold_in(jax.random.fold_in(seeds[13], part), 71), part)
    page_index = draw_page_index(jax.random.fold_in(jax.random.fold_in(seeds[13], part), 71), part)
    lengths = draw_lengths(jax.random.fold_in(jax.random.fold_in(seeds[13], part), 71), part)
    queries = draw_queries(jax.random.fold_in(jax.random.fold_in(seeds[13], part), 71), part)
    new_latent = draw_new_latent(jax.random.fold_in(jax.random.fold_in(seeds[13], part), 71), part)
    up_value = gaussian(seeds[6], (HEADS, CKV, VDIM), CKV ** -0.5, 0.25, ((0, 4),))
    out_proj = gaussian(seeds[7], (HEADS * VDIM, D), (HEADS * VDIM) ** -0.5, 0.0625, ((0, 4), (1, 4)))
    residual = draw_residual(jax.random.fold_in(jax.random.fold_in(seeds[13], part), 71), part)
    norm_gain = jnp.clip(1.0 + 0.18 * jax.random.normal(seeds[9], (D,), jnp.float32), 0.1, 1.9)
    w_gate = gaussian(seeds[10], (D, FF), D ** -0.5, 0.0625, ((0, 4), (1, 4)))
    w_up = gaussian(seeds[11], (D, FF), D ** -0.5, 0.0625, ((0, 4), (1, 4)))
    w_down = gaussian(seeds[12], (FF, D), FF ** -0.5, 0.0546875, ((0, 4), (1, 4)))
    return {"latent_store": latent_store, "page_rank": page_rank, "page_index": page_index, "lengths": lengths, "queries": queries, "new_latent": new_latent, "up_value": up_value, "out_proj": out_proj, "residual": residual, "norm_gain": norm_gain, "w_gate": w_gate, "w_up": w_up, "w_down": w_down}


score_scale = 1.0 / 192.0 ** 0.5
epsilon = 1e-06
mask_value = -1e+30

def reference(latent_store, page_rank, page_index, lengths, queries, new_latent, up_value, out_proj, residual, norm_gain, w_gate, w_up, w_down):
    slot_ids = jnp.arange(QSLOTS, dtype=jnp.int32)
    store_base = (slot_ids // SLOT_DEV * SLOT_DEV).astype(jnp.int32)
    query_all = queries.reshape(RANKS, REQ_DP, STEPS, HEADS, LAT)
    fresh_all = new_latent.reshape(RANKS, REQ_DP, STEPS, LAT)

    def one_rank(inputs):
        rank_row, index_row, length_row, query_rank, fresh_rank = inputs
        pages = latent_store[rank_row.astype(jnp.int32), store_base + index_row.astype(jnp.int32)]
        context = pages.reshape(REQ_DP, PAGES, LAT, PAGE).transpose(0, 2, 1, 3).reshape(REQ_DP, LAT, PAGES * PAGE).astype(jnp.float32)
        query_f = query_rank.astype(jnp.float32)
        fresh_f = fresh_rank.astype(jnp.float32)
        context_scores = jnp.einsum('jshl,jlt->jsht', query_f, context) * score_scale
        positions = jnp.arange(PAGES * PAGE, dtype=jnp.int32)
        seen = (positions[None, :] < length_row[:, None])[:, None, None, :]
        context_scores = jnp.where(seen, context_scores, mask_value)
        fresh_scores = jnp.einsum('jshl,jul->jshu', query_f, fresh_f) * score_scale
        step_ids = jnp.arange(STEPS, dtype=jnp.int32)
        fresh_seen = (step_ids[None, :] <= step_ids[:, None])[None, :, None, :]
        fresh_scores = jnp.where(fresh_seen, fresh_scores, mask_value)
        highest = jnp.maximum(lax.optimization_barrier(jnp.max(context_scores, axis=3)), lax.optimization_barrier(jnp.max(fresh_scores, axis=3)))
        context_weights = jnp.where(seen, jnp.exp(context_scores - highest[..., None]), 0.0)
        fresh_weights = jnp.where(fresh_seen, jnp.exp(fresh_scores - highest[..., None]), 0.0)
        denominator = lax.optimization_barrier(jnp.sum(context_weights, axis=3)) + lax.optimization_barrier(jnp.sum(fresh_weights, axis=3))
        context_rounded = lax.optimization_barrier(context_weights.astype(jnp.bfloat16)).astype(jnp.float32)
        fresh_rounded = lax.optimization_barrier(fresh_weights.astype(jnp.bfloat16)).astype(jnp.float32)
        combined = jnp.einsum('jsht,jct->jshc', context_rounded, context[:, :CKV, :])
        combined = combined + jnp.einsum('jshu,juc->jshc', fresh_rounded, fresh_f[:, :, :CKV])
        return (combined / denominator[..., None]).astype(jnp.bfloat16)
    attention = lax.map(one_rank, (page_rank, page_index, lengths, query_all, fresh_all))
    attention = attention.reshape(ROWS, HEADS, CKV)
    head_values = jnp.einsum('rhc,hcv->rhv', attention.astype(jnp.float32), up_value.astype(jnp.float32))
    head_values = head_values.astype(jnp.bfloat16).reshape(ROWS, HEADS * VDIM)
    attn_out = jnp.dot(head_values, out_proj, preferred_element_type=jnp.float32)
    mixed = residual.astype(jnp.float32) + attn_out
    squares = lax.optimization_barrier(jnp.mean(mixed * mixed, axis=1, keepdims=True))
    normed = (mixed * lax.rsqrt(squares + epsilon) * norm_gain).astype(jnp.bfloat16)
    gate = jnp.dot(normed, w_gate, preferred_element_type=jnp.float32)
    up_part = jnp.dot(normed, w_up, preferred_element_type=jnp.float32)
    hidden = (jax.nn.silu(gate) * up_part).astype(jnp.bfloat16)
    return (mixed + jnp.dot(hidden, w_down, preferred_element_type=jnp.float32)).astype(jnp.bfloat16)
```

```python
import functools
import math

import jax
import jax.numpy as jnp
from jax import lax
from jax.experimental import pallas as pl
from jax.experimental.pallas import tpu as pltpu
from jax.sharding import PartitionSpec as P

CKV = 512
PAGE = 128
PAGES = 48
LANES = 128
MIB = 1 << 20

score_scale = 1.0 / math.sqrt(192.0)
epsilon = 1e-06
mask_value = -1e30


def merged_2(array, axis, join):
    gathered = jax.tree.map(
        lambda a, kind: lax.all_gather(a.astype(kind), axis),
        array,
        jax.tree.map(lambda a: jnp.bfloat16 if a.dtype == jnp.float32 else a.dtype, array),
    )

    def take(source):
        return jax.tree.map(
            lambda a, own: lax.dynamic_index_in_dim(a, source, 0, False).astype(own.dtype),
            gathered,
            array,
        )

    return lax.fori_loop(
        1, lax.axis_size(axis), lambda source, state: join(state, take(source)), take(0)
    )


def page_partials(page_keys, page_queries, key_counts):
    scores = (
        jnp.einsum("pshl,plt->psht", page_queries, page_keys, preferred_element_type=jnp.float32)
        * score_scale
    )
    places = lax.broadcasted_iota(jnp.int32, scores.shape, 3)
    visible = places < key_counts[:, None, None, None]
    scores = jnp.where(visible, scores, mask_value)
    row_peak = jnp.max(scores, axis=3)
    weights = jnp.where(visible, jnp.exp(scores - row_peak[..., None]), 0.0)
    row_total = jnp.sum(weights, axis=3)
    partial_value = jnp.einsum(
        "psht,pct->pshc",
        weights.astype(jnp.bfloat16),
        page_keys[:, :CKV, :],
        preferred_element_type=jnp.float32,
    )
    return (partial_value, row_peak, row_total)


def join_pages(partial_value, row_peak, row_total, slot_request, requests):
    owner_mask = slot_request[None, :] == jnp.arange(requests, dtype=jnp.int32)[:, None]
    spread = owner_mask[:, :, None, None]
    best_peak = jnp.max(jnp.where(spread, row_peak[None], mask_value), axis=1)
    factor = jnp.where(spread, jnp.exp(row_peak[None] - best_peak[:, None]), 0.0)
    joined = jnp.einsum("jpsh,pshc->jshc", factor, partial_value, precision=lax.Precision.HIGHEST)
    summed = jnp.sum(factor * row_total[None], axis=1)
    return (joined, best_peak, summed)


def combine(former, latter):
    former_sum, former_peak, former_total = former
    latter_sum, latter_peak, latter_total = latter
    highest = jnp.maximum(former_peak, latter_peak)
    former_scale = jnp.exp(former_peak - highest)
    latter_scale = jnp.exp(latter_peak - highest)
    merged_sum = former_sum * former_scale[..., None] + latter_sum * latter_scale[..., None]
    return (merged_sum, highest, former_total * former_scale + latter_total * latter_scale)


def fresh_partial(query_rows, fresh_rows, active):
    scores = (
        jnp.einsum("jshl,jul->jshu", query_rows, fresh_rows, preferred_element_type=jnp.float32)
        * score_scale
    )
    step_query = lax.broadcasted_iota(jnp.int32, scores.shape, 1)
    step_key = lax.broadcasted_iota(jnp.int32, scores.shape, 3)
    visible = (step_key <= step_query) & active
    scores = jnp.where(visible, scores, mask_value)
    row_peak = jnp.max(scores, axis=3)
    weights = jnp.where(visible, jnp.exp(scores - row_peak[..., None]), 0.0)
    row_total = jnp.sum(weights, axis=3)
    partial_value = jnp.einsum(
        "jshu,juc->jshc",
        weights.astype(jnp.bfloat16),
        fresh_rows[:, :, :CKV],
        preferred_element_type=jnp.float32,
    )
    return (partial_value, row_peak, row_total)


def pages_moved(
    latent_store,
    page_rank,
    page_index,
    lengths,
    queries,
    new_latent,
    up_value,
    out_proj,
    residual,
    norm_gain,
    w_gate,
    w_up,
    w_down,
):
    my_rank = lax.axis_index("dp")
    my_column = lax.axis_index("rep")
    rank_count, slot_count = page_rank.shape
    capacity = (slot_count + rank_count - 1) // rank_count
    requests = lengths.shape[1]
    rows_here = residual.shape[0]
    steps_count = rows_here // requests
    latent_width = new_latent.shape[1]
    head_count = queries.shape[1] // latent_width
    query_rows = queries.reshape(requests, steps_count, head_count, latent_width)
    fresh_rows = new_latent.reshape(requests, steps_count, latent_width)
    slot_order = jnp.arange(slot_count, dtype=jnp.int32)
    request_ids = jnp.arange(requests, dtype=jnp.int32)
    cap_ids = jnp.arange(capacity, dtype=jnp.int32)
    global_slot = my_column * slot_count + slot_order
    slot_request = global_slot // PAGES
    slot_page = global_slot % PAGES
    own_lengths = lax.dynamic_index_in_dim(lengths, my_rank, 0, keepdims=False)
    slot_length = jnp.sum(
        jnp.where(slot_request[:, None] == request_ids[None, :], own_lengths[None, :], 0), axis=1
    )
    key_counts = jnp.clip(slot_length - slot_page * PAGE, 0, PAGE)
    my_sources = lax.dynamic_index_in_dim(page_rank, my_rank, 0, keepdims=False)
    earlier = (my_sources[None, :] == my_sources[:, None]) & (
        slot_order[None, :] < slot_order[:, None]
    )
    arrival_rank = jnp.sum(earlier.astype(jnp.int32), axis=1)
    arrival_slot = my_sources * capacity + arrival_rank
    held_here = page_rank == my_rank
    held_order = jnp.cumsum(held_here.astype(jnp.int32), axis=1) - 1
    selector = held_here[:, None, :] & (held_order[:, None, :] == cap_ids[None, :, None])
    sent_valid = jnp.any(selector, axis=2).reshape(-1)
    sent_page = jnp.sum(jnp.where(selector, page_index[:, None, :], 0), axis=2).reshape(-1)
    stored = latent_store[0]
    outgoing = jnp.take(stored, sent_page, axis=0)
    outgoing = jnp.where(sent_valid[:, None, None], outgoing, jnp.zeros_like(outgoing))
    arrived = lax.all_to_all(outgoing, "dp", split_axis=0, concat_axis=0, tiled=True)
    restored = jnp.take(arrived, arrival_slot, axis=0)
    page_queries = jnp.take(query_rows, slot_request, axis=0)
    partial_value, row_peak, row_total = page_partials(restored, page_queries, key_counts)
    joined = join_pages(partial_value, row_peak, row_total, slot_request, requests)
    local_part = combine(joined, fresh_partial(query_rows, fresh_rows, my_column == 0))
    merged = merged_2(local_part, "rep", combine)
    attention = (
        (merged[0] / merged[2][..., None]).astype(jnp.bfloat16).reshape(rows_here, head_count, CKV)
    )
    headed = lax.all_to_all(attention, "dp", split_axis=1, concat_axis=0, tiled=True)
    values = jnp.einsum("rhc,hcv->rhv", headed, up_value, preferred_element_type=jnp.float32)
    values = values.astype(jnp.bfloat16).reshape(headed.shape[0], -1)
    picked = values
    attn_out = lax.psum_scatter(
        jnp.dot(picked, out_proj, preferred_element_type=jnp.float32).astype(jnp.bfloat16),
        "dp",
        scatter_dimension=0,
        tiled=True,
    ).astype(jnp.float32)
    mixed_rows = residual.astype(jnp.float32) + attn_out
    squares = lax.psum(jnp.sum(mixed_rows * mixed_rows, axis=1), "rep")
    normed = (mixed_rows * lax.rsqrt(squares / (norm_gain.shape[0] * lax.axis_size("rep")) + epsilon)[:, None] * norm_gain).astype(
        jnp.bfloat16
    )
    piece = lax.all_gather(normed, "dp", axis=0, tiled=True)
    gate_part = jnp.dot(piece, w_gate, preferred_element_type=jnp.float32)
    up_part = jnp.dot(piece, w_up, preferred_element_type=jnp.float32)
    partial_rows = jnp.concatenate([gate_part, up_part], axis=1)
    gate_up = lax.psum(partial_rows.astype(jnp.bfloat16), "rep").astype(jnp.float32)
    hidden_width = w_gate.shape[1]
    hidden = (jax.nn.silu(gate_up[:, :hidden_width]) * gate_up[:, hidden_width:]).astype(
        jnp.bfloat16
    )
    picked = hidden
    mlp_out = lax.psum_scatter(
        jnp.dot(picked, w_down, preferred_element_type=jnp.float32).astype(jnp.bfloat16),
        "dp",
        scatter_dimension=0,
        tiled=True,
    ).astype(jnp.float32)
    return (mixed_rows + mlp_out).astype(jnp.bfloat16)


def partners(array, axis):
    size = lax.axis_size(axis)
    return [
        lax.ppermute(array, axis, [(i, i ^ step) for i in range(size)]) for step in range(1, size)
    ]


def thirds(value):
    high = value.astype(jnp.bfloat16).astype(jnp.float32)
    rest = value - high
    middle = rest.astype(jnp.bfloat16).astype(jnp.float32)
    return high, middle, (rest - middle).astype(jnp.bfloat16).astype(jnp.float32)


def lane_ids(rows):
    return lax.broadcasted_iota(jnp.int32, (rows, LANES), 1)


def smem():
    return pl.BlockSpec(memory_space=pltpu.SMEM)


def vmem():
    return pl.BlockSpec(memory_space=pltpu.VMEM)


def locate_kernel(capacity, slots, place, lengths, rank_near, index_near, rank_far, index_far, page, count):
    me, column = place[0], place[1]
    ranks = lengths.shape[0]
    for step in range(ranks):
        rank = me ^ step
        length = lengths[rank, 0]
        for side, (table, index) in enumerate(((rank_near, index_near), (rank_far, index_far))):
            first = (step * 2 + side) * capacity
            for k in range(capacity):
                page[first + k] = 0
                count[first + k] = 0
            base = (column ^ side) * slots

            def visit(slot, found):
                here = table[rank, slot] == me

                @pl.when(here)
                def _():
                    page[first + found] = index[rank, slot]
                    start = ((base + slot) % PAGES) * PAGE
                    count[first + found] = jnp.clip(length - start, 0, PAGE)

                return found + here.astype(jnp.int32)

            lax.fori_loop(0, slots, visit, 0)


def attend_kernel(capacity, heads, place, page, count, *refs):
    ranks = (len(refs) - 4) // 2
    query_refs, (near, far, fresh) = refs[:ranks], refs[ranks : ranks + 3]
    out_refs, held = refs[ranks + 3 : -1], refs[-1]
    me, column = place[0], place[1]
    rows = query_refs[0].shape[0]
    steps = rows // (ranks * heads)
    lanes = lane_ids(rows)
    across = (((1,), (1,)), ((), ()))
    for step in range(ranks):
        rank = me ^ step
        query = query_refs[step][...]
        scores, values = [], []
        for side, pages in enumerate((near, far)):
            for k in range(capacity):
                place_of = (step * 2 + side) * capacity + k
                keys = pages.at[page[place_of]]
                score = jnp.dot(query, keys[...], preferred_element_type=jnp.float32) * score_scale
                scores.append(jnp.where(lanes < count[place_of], score, mask_value))
                values.append(keys)
        peak = functools.reduce(jnp.maximum, scores)
        row_peak = jnp.max(peak, axis=1, keepdims=True)
        if step == 0:
            recent = lax.dot_general(
                query, fresh[...], across, preferred_element_type=jnp.float32
            ) * score_scale
            width = recent.shape[1]
            key = lax.broadcasted_iota(jnp.int32, (rows, width), 1)
            row_step = lax.broadcasted_iota(jnp.int32, (rows, width), 0) // (ranks * heads)
            seen = (key <= row_step) & (column < 2)
            recent = jnp.where(seen, recent, mask_value)
            row_peak = jnp.maximum(row_peak, jnp.max(recent, axis=1, keepdims=True))
        total, summed = None, None
        for score, keys in zip(scores, values):
            weight = jnp.where(score > 0.5 * mask_value, jnp.exp(score - row_peak), 0.0)
            total = weight if total is None else total + weight
            part = lax.dot_general(
                weight.astype(jnp.bfloat16), keys[0:CKV, :], across, preferred_element_type=jnp.float32
            )
            summed = part if summed is None else summed + part
        row_total = jnp.sum(total, axis=1, keepdims=True)
        if step == 0:
            weight = jnp.where(seen, jnp.exp(recent - row_peak), 0.0)
            row_total = row_total + jnp.sum(weight, axis=1, keepdims=True)
            summed = summed + jnp.dot(
                weight.astype(jnp.bfloat16), fresh[:, 0:CKV], preferred_element_type=jnp.float32
            )
        extra = jnp.zeros((rows, LANES), jnp.float32)
        for lane, part in enumerate(thirds(row_peak) + thirds(row_total)):
            extra = jnp.where(lanes == lane, part, extra)
        held[:, 0:CKV] = summed
        held[:, CKV:] = extra
        for far_step, out in enumerate(out_refs):
            target = me ^ far_step
            block = [
                held[pl.ds(pl.multiple_of((u * ranks + target) * heads, heads), heads), :]
                for u in range(steps)
            ]
            start = pl.multiple_of(rank * steps * heads, steps * heads)
            out[pl.ds(start, steps * heads), :] = jnp.concatenate(block, axis=0).astype(jnp.bfloat16)


def lift_kernel(heads, ranks, place, *refs):
    parts, up_value, out, joined, tall = refs[:ranks], refs[ranks], refs[ranks + 1], refs[-2], refs[-1]
    count = parts[0].shape[0]
    rows = count // heads
    core = place[1] % 2
    blocks = [part[...].astype(jnp.float32) for part in parts]
    peaks = [b[:, CKV : CKV + 1] + b[:, CKV + 1 : CKV + 2] + b[:, CKV + 2 : CKV + 3] for b in blocks]
    totals = [b[:, CKV + 3 : CKV + 4] + b[:, CKV + 4 : CKV + 5] + b[:, CKV + 5 : CKV + 6] for b in blocks]
    peak = functools.reduce(jnp.maximum, peaks)
    value, total = 0.0, 0.0
    for block, own_peak, own_total in zip(blocks, peaks, totals):
        factor = jnp.exp(own_peak - peak)
        value = value + block[:, 0:CKV] * factor
        total = total + own_total * factor
    for group in range(CKV // LANES):
        joined[group] = value[:, group * LANES : (group + 1) * LANES]
    lanes = lane_ids(count)
    tall[...] = jnp.where(lanes < 3 * heads, peak, total)
    lanes = lane_ids(rows)
    extra = jnp.zeros((rows, LANES), jnp.float32)
    for head in range(heads):
        pick = pl.ds(head, rows, stride=heads)
        out[:, head * LANES : (head + 1) * LANES] = jnp.dot(
            jnp.concatenate([joined[g, pick, :] for g in range(CKV // LANES)], axis=1).astype(jnp.bfloat16),
            up_value[core * heads + head],
            preferred_element_type=jnp.float32,
        ).astype(jnp.bfloat16)
        extra = jnp.where(lanes % heads == head, tall[pick, :], extra)
    high, middle, low = thirds(extra)
    piece = lanes // heads % 3
    out[:, heads * LANES :] = jnp.where(
        piece == 0, high, jnp.where(piece == 1, middle, low)
    ).astype(jnp.bfloat16)


def project_kernel(heads, reps, place, *refs):
    parts, (out_proj, own_rows, sent, kept) = refs[:reps], refs[reps:]
    core = place[1] % 2
    width = heads * LANES
    result = own_rows[...]
    for side in range(2):
        blocks = [parts[step][...].astype(jnp.float32) for step in range(side, reps, 2)]
        tails = [b[:, width:] for b in blocks]

        def whole(tail, first):
            at = [pltpu.roll(tail, LANES - (first + k) * heads, 1) if first + k else tail for k in range(3)]
            return at[0] + at[1] + at[2]

        peaks = [whole(tail, 0) for tail in tails]
        totals = [whole(tail, 3) for tail in tails]
        live = lane_ids(result.shape[0]) < heads
        peaks = [jnp.where(live, p, 0.0) for p in peaks]
        totals = [jnp.where(live, t, 1.0) for t in totals]
        peak = functools.reduce(jnp.maximum, peaks)
        factors = [jnp.exp(p - peak) for p in peaks]
        total = sum(f * t for f, t in zip(factors, totals))
        factors = [f / total for f in factors]
        mixed = []
        for head in range(heads):
            lane = slice(head * LANES, (head + 1) * LANES)
            mixed.append(sum(b[:, lane] * f[:, head : head + 1] for b, f in zip(blocks, factors)))
        values = jnp.concatenate(mixed, axis=1).astype(jnp.bfloat16)
        start = pl.multiple_of((core ^ side) * width, width)
        result = result + jnp.dot(
            values, out_proj[pl.ds(start, width), :], preferred_element_type=jnp.float32
        )
    kept[...] = result
    sent[...] = result.astype(jnp.bfloat16)


def gate_kernel(ranks, *refs):
    kept, others, (gain, w_gate, w_up, out, mixed_out) = refs[0], refs[1:ranks], refs[ranks:]
    mixed = kept[...]
    for other in others:
        mixed = mixed + other[...].astype(jnp.float32)
    mixed_out[...] = mixed
    scaled = (mixed * gain[...]).astype(jnp.bfloat16)
    width = w_gate.shape[1]
    out[:, 0:width] = jnp.dot(scaled, w_gate[...], preferred_element_type=jnp.float32).astype(jnp.bfloat16)
    out[:, width : 2 * width] = jnp.dot(scaled, w_up[...], preferred_element_type=jnp.float32).astype(
        jnp.bfloat16
    )
    squares = jnp.sum(mixed * mixed, axis=1, keepdims=True)
    lanes = lane_ids(mixed.shape[0])
    extra = jnp.zeros(lanes.shape, jnp.float32)
    for lane, part in enumerate(thirds(squares)):
        extra = jnp.where(lanes == lane, part, extra)
    out[:, 2 * width :] = extra.astype(jnp.bfloat16)


def down_kernel(reps, model_width, *refs):
    parts, (w_down, out) = refs[:reps], refs[reps:]
    width = w_down.shape[0]
    total = parts[0][...].astype(jnp.float32)
    for part in parts[1:]:
        total = total + part[...].astype(jnp.float32)
    tail = total[:, 2 * width :]
    squares = jnp.sum(jnp.where(lane_ids(tail.shape[0]) < 3, tail, 0.0), axis=1, keepdims=True)
    scale = lax.rsqrt(squares / model_width + epsilon)
    gate = total[:, 0:width] * scale
    hidden = (jax.nn.silu(gate) * (total[:, width : 2 * width] * scale)).astype(jnp.bfloat16)
    out[...] = jnp.dot(hidden, w_down[...], preferred_element_type=jnp.float32).astype(jnp.bfloat16)


def call(kernel, name, operands, specs, outputs, limit, flops=0, moved=0, scratch=(), out_specs=None):
    return pl.pallas_call(
        kernel,
        name=name,
        out_shape=outputs,
        in_specs=specs,
        out_specs=jax.tree.map(lambda _: vmem(), outputs) if out_specs is None else out_specs,
        scratch_shapes=list(scratch),
        compiler_params=pltpu.CompilerParams(vmem_limit_bytes=limit),
        cost_estimate=pl.CostEstimate(flops=flops, bytes_accessed=moved, transcendentals=0),
    )(*operands)


def shape_of(shape, dtype=jnp.bfloat16):
    return jax.ShapeDtypeStruct(shape, dtype)


def queries_moved(
    latent_store,
    page_rank,
    page_index,
    lengths,
    queries,
    new_latent,
    up_value,
    out_proj,
    residual,
    norm_gain,
    w_gate,
    w_up,
    w_down,
):
    ranks, reps = lax.axis_size("dp"), lax.axis_size("rep")
    me, column = lax.axis_index("dp"), lax.axis_index("rep")
    slots = page_rank.shape[1]
    capacity = (slots + ranks - 1) // ranks
    steps, columns = residual.shape
    latent = new_latent.shape[1]
    head_count = queries.shape[1] // latent
    heads = head_count // (2 * ranks)
    rows = ranks * steps
    core_pairs = [(i, i ^ 1) for i in range(reps)]
    place = jnp.stack([me, column])

    share = lax.dynamic_index_in_dim(
        queries.reshape(steps, ranks, 2, heads * latent), column % 2, 2, keepdims=False
    )
    arrived = [share] + partners(share, "dp")
    near = latent_store[0]
    far = lax.ppermute(near, "rep", core_pairs)
    tables = lax.ppermute(jnp.stack([page_rank, page_index]), "rep", core_pairs)
    found = 2 * ranks * capacity
    page, count = call(
        functools.partial(locate_kernel, capacity, slots),
        "locate",
        (place, lengths, page_rank, page_index, tables[0], tables[1]),
        [smem()] * 6,
        [shape_of((found,), jnp.int32)] * 2,
        4 * MIB,
        out_specs=[smem()] * 2,
    )
    fresh = jnp.concatenate([new_latent, jnp.zeros((8 - steps, latent), new_latent.dtype)])
    own_rows = jnp.where(
        (jnp.arange(rows) // steps == me)[:, None], jnp.tile(residual.astype(jnp.float32), (ranks, 1)), 0.0
    )
    query_rows = [a.reshape(steps * ranks * heads, latent) for a in arrived]
    width = CKV + LANES
    partial_rows = call(
        functools.partial(attend_kernel, capacity, heads),
        "attend",
        (place, page, count, *query_rows, near, far, fresh),
        [smem()] * 3 + [vmem()] * (ranks + 3),
        [shape_of((rows * heads, width))] * ranks,
        12 * MIB,
        scratch=[pltpu.VMEM((steps * ranks * heads, width), jnp.float32)],
        flops=2 * 2 * slots * PAGE * rows * heads * latent,
        moved=2 * near.size * 2,
    )
    joined = [partial_rows[0]] + [
        lax.ppermute(partial_rows[s], "dp", [(i, i ^ s) for i in range(ranks)]) for s in range(1, ranks)
    ]
    lifted = call(
        functools.partial(lift_kernel, heads, ranks),
        "lift",
        (place, *joined, up_value),
        [smem()] + [vmem()] * (ranks + 1),
        shape_of((rows, (heads + 1) * LANES)),
        8 * MIB,
        scratch=[
            pltpu.VMEM((CKV // LANES, rows * heads, LANES), jnp.float32),
            pltpu.VMEM((rows * heads, LANES), jnp.float32),
        ],
        flops=2 * rows * heads * CKV * LANES,
        moved=up_value.size * 2,
    )
    sent, kept = call(
        functools.partial(project_kernel, heads, reps),
        "project",
        (place, lifted, *partners(lifted, "rep"), out_proj, own_rows),
        [smem()] + [vmem()] * (reps + 2),
        [shape_of((rows, columns)), shape_of((rows, columns), jnp.float32)],
        12 * MIB,
        flops=2 * rows * out_proj.size,
        moved=out_proj.size * 2,
    )
    gate_up, mixed = call(
        functools.partial(gate_kernel, ranks),
        "gate",
        (kept, *partners(sent, "dp"), norm_gain.reshape(1, columns), w_gate, w_up),
        [vmem()] * (ranks + 3),
        [shape_of((rows, 2 * w_gate.shape[1] + LANES)), shape_of((rows, columns), jnp.float32)],
        28 * MIB,
        flops=4 * rows * w_gate.size,
        moved=w_gate.size * 4,
    )
    down = call(
        functools.partial(down_kernel, reps, columns * reps),
        "down",
        (gate_up, *partners(gate_up, "rep"), w_down),
        [vmem()] * (reps + 1),
        shape_of((rows, columns)),
        16 * MIB,
        flops=2 * rows * w_down.size,
        moved=w_down.size * 2,
    )

    def mine(array):
        return lax.dynamic_slice_in_dim(array, me * steps, steps).astype(jnp.float32)

    return (mine(mixed) + sum(mine(a) for a in [down] + partners(down, "dp"))).astype(jnp.bfloat16)


def on_device(*arrays):
    ranks = lax.axis_size("dp")
    lengths, queries, new_latent = arrays[3:6]
    heads = queries.shape[1] // new_latent.shape[1]
    if ranks <= 8 and heads % (16 * ranks) == 0 and lengths.shape[1] == 1:
        return queries_moved(*arrays)
    return pages_moved(*arrays)


def solution(mesh):
    in_specs = (
        P(("groups", "dp"), "rep", None, None),
        P("groups", "rep"),
        P("groups", "rep"),
        P("groups", None),
        P(("groups", "dp"), None),
        P(("groups", "dp"), None),
        P("dp", None, None),
        P("dp", "rep"),
        P(("groups", "dp"), "rep"),
        P("rep"),
        P("rep", "dp"),
        P("rep", "dp"),
        P("dp", "rep"),
    )
    out_specs = P(("groups", "dp"), "rep")
    return jax.shard_map(
        on_device, mesh=mesh, in_specs=in_specs, out_specs=out_specs, check_vma=False
    )
```

```python
import functools
import math

import jax
import jax.numpy as jnp
from jax import lax
from jax.experimental import pallas as pl
from jax.experimental.pallas import tpu as pltpu
from jax.sharding import PartitionSpec as P

CKV = 512
PAGE = 128
PAGES = 48
LANES = 128
MIB = 1 << 20

score_scale = 1.0 / math.sqrt(192.0)
epsilon = 1e-06
mask_value = -1e30


def merged_2(array, axis, join):
    gathered = jax.tree.map(
        lambda a, kind: lax.all_gather(a.astype(kind), axis),
        array,
        jax.tree.map(lambda a: jnp.bfloat16 if a.dtype == jnp.float32 else a.dtype, array),
    )

    def take(source):
        return jax.tree.map(
            lambda a, own: lax.dynamic_index_in_dim(a, source, 0, False).astype(own.dtype),
            gathered,
            array,
        )

    return lax.fori_loop(
        1, lax.axis_size(axis), lambda source, state: join(state, take(source)), take(0)
    )


def page_partials(page_keys, page_queries, key_counts):
    scores = (
        jnp.einsum("pshl,plt->psht", page_queries, page_keys, preferred_element_type=jnp.float32)
        * score_scale
    )
    places = lax.broadcasted_iota(jnp.int32, scores.shape, 3)
    visible = places < key_counts[:, None, None, None]
    scores = jnp.where(visible, scores, mask_value)
    row_peak = jnp.max(scores, axis=3)
    weights = jnp.where(visible, jnp.exp(scores - row_peak[..., None]), 0.0)
    row_total = jnp.sum(weights, axis=3)
    partial_value = jnp.einsum(
        "psht,pct->pshc",
        weights.astype(jnp.bfloat16),
        page_keys[:, :CKV, :],
        preferred_element_type=jnp.float32,
    )
    return (partial_value, row_peak, row_total)


def join_pages(partial_value, row_peak, row_total, slot_request, requests):
    owner_mask = slot_request[None, :] == jnp.arange(requests, dtype=jnp.int32)[:, None]
    spread = owner_mask[:, :, None, None]
    best_peak = jnp.max(jnp.where(spread, row_peak[None], mask_value), axis=1)
    factor = jnp.where(spread, jnp.exp(row_peak[None] - best_peak[:, None]), 0.0)
    joined = jnp.einsum("jpsh,pshc->jshc", factor, partial_value, precision=lax.Precision.HIGHEST)
    summed = jnp.sum(factor * row_total[None], axis=1)
    return (joined, best_peak, summed)


def combine(former, latter):
    former_sum, former_peak, former_total = former
    latter_sum, latter_peak, latter_total = latter
    highest = jnp.maximum(former_peak, latter_peak)
    former_scale = jnp.exp(former_peak - highest)
    latter_scale = jnp.exp(latter_peak - highest)
    merged_sum = former_sum * former_scale[..., None] + latter_sum * latter_scale[..., None]
    return (merged_sum, highest, former_total * former_scale + latter_total * latter_scale)


def fresh_partial(query_rows, fresh_rows, active):
    scores = (
        jnp.einsum("jshl,jul->jshu", query_rows, fresh_rows, preferred_element_type=jnp.float32)
        * score_scale
    )
    step_query = lax.broadcasted_iota(jnp.int32, scores.shape, 1)
    step_key = lax.broadcasted_iota(jnp.int32, scores.shape, 3)
    visible = (step_key <= step_query) & active
    scores = jnp.where(visible, scores, mask_value)
    row_peak = jnp.max(scores, axis=3)
    weights = jnp.where(visible, jnp.exp(scores - row_peak[..., None]), 0.0)
    row_total = jnp.sum(weights, axis=3)
    partial_value = jnp.einsum(
        "jshu,juc->jshc",
        weights.astype(jnp.bfloat16),
        fresh_rows[:, :, :CKV],
        preferred_element_type=jnp.float32,
    )
    return (partial_value, row_peak, row_total)


def pages_moved(
    latent_store,
    page_rank,
    page_index,
    lengths,
    queries,
    new_latent,
    up_value,
    out_proj,
    residual,
    norm_gain,
    w_gate,
    w_up,
    w_down,
):
    my_rank = lax.axis_index("dp")
    my_column = lax.axis_index("rep")
    rank_count, slot_count = page_rank.shape
    capacity = (slot_count + rank_count - 1) // rank_count
    requests = lengths.shape[1]
    rows_here = residual.shape[0]
    steps_count = rows_here // requests
    latent_width = new_latent.shape[1]
    head_count = queries.shape[1] // latent_width
    query_rows = queries.reshape(requests, steps_count, head_count, latent_width)
    fresh_rows = new_latent.reshape(requests, steps_count, latent_width)
    slot_order = jnp.arange(slot_count, dtype=jnp.int32)
    request_ids = jnp.arange(requests, dtype=jnp.int32)
    cap_ids = jnp.arange(capacity, dtype=jnp.int32)
    global_slot = my_column * slot_count + slot_order
    slot_request = global_slot // PAGES
    slot_page = global_slot % PAGES
    own_lengths = lax.dynamic_index_in_dim(lengths, my_rank, 0, keepdims=False)
    slot_length = jnp.sum(
        jnp.where(slot_request[:, None] == request_ids[None, :], own_lengths[None, :], 0), axis=1
    )
    key_counts = jnp.clip(slot_length - slot_page * PAGE, 0, PAGE)
    my_sources = lax.dynamic_index_in_dim(page_rank, my_rank, 0, keepdims=False)
    earlier = (my_sources[None, :] == my_sources[:, None]) & (
        slot_order[None, :] < slot_order[:, None]
    )
    arrival_rank = jnp.sum(earlier.astype(jnp.int32), axis=1)
    arrival_slot = my_sources * capacity + arrival_rank
    held_here = page_rank == my_rank
    held_order = jnp.cumsum(held_here.astype(jnp.int32), axis=1) - 1
    selector = held_here[:, None, :] & (held_order[:, None, :] == cap_ids[None, :, None])
    sent_valid = jnp.any(selector, axis=2).reshape(-1)
    sent_page = jnp.sum(jnp.where(selector, page_index[:, None, :], 0), axis=2).reshape(-1)
    stored = latent_store[0]
    outgoing = jnp.take(stored, sent_page, axis=0)
    outgoing = jnp.where(sent_valid[:, None, None], outgoing, jnp.zeros_like(outgoing))
    arrived = lax.all_to_all(outgoing, "dp", split_axis=0, concat_axis=0, tiled=True)
    restored = jnp.take(arrived, arrival_slot, axis=0)
    page_queries = jnp.take(query_rows, slot_request, axis=0)
    partial_value, row_peak, row_total = page_partials(restored, page_queries, key_counts)
    joined = join_pages(partial_value, row_peak, row_total, slot_request, requests)
    local_part = combine(joined, fresh_partial(query_rows, fresh_rows, my_column == 0))
    merged = merged_2(local_part, "rep", combine)
    attention = (
        (merged[0] / merged[2][..., None]).astype(jnp.bfloat16).reshape(rows_here, head_count, CKV)
    )
    headed = lax.all_to_all(attention, "dp", split_axis=1, concat_axis=0, tiled=True)
    values = jnp.einsum("rhc,hcv->rhv", headed, up_value, preferred_element_type=jnp.float32)
    values = values.astype(jnp.bfloat16).reshape(headed.shape[0], -1)
    picked = values
    attn_out = lax.psum_scatter(
        jnp.dot(picked, out_proj, preferred_element_type=jnp.float32).astype(jnp.bfloat16),
        "dp",
        scatter_dimension=0,
        tiled=True,
    ).astype(jnp.float32)
    mixed_rows = residual.astype(jnp.float32) + attn_out
    squares = lax.psum(jnp.sum(mixed_rows * mixed_rows, axis=1), "rep")
    normed = (mixed_rows * lax.rsqrt(squares / (norm_gain.shape[0] * lax.axis_size("rep")) + epsilon)[:, None] * norm_gain).astype(
        jnp.bfloat16
    )
    piece = lax.all_gather(normed, "dp", axis=0, tiled=True)
    gate_part = jnp.dot(piece, w_gate, preferred_element_type=jnp.float32)
    up_part = jnp.dot(piece, w_up, preferred_element_type=jnp.float32)
    partial_rows = jnp.concatenate([gate_part, up_part], axis=1)
    gate_up = lax.psum(partial_rows.astype(jnp.bfloat16), "rep").astype(jnp.float32)
    hidden_width = w_gate.shape[1]
    hidden = (jax.nn.silu(gate_up[:, :hidden_width]) * gate_up[:, hidden_width:]).astype(
        jnp.bfloat16
    )
    picked = hidden
    mlp_out = lax.psum_scatter(
        jnp.dot(picked, w_down, preferred_element_type=jnp.float32).astype(jnp.bfloat16),
        "dp",
        scatter_dimension=0,
        tiled=True,
    ).astype(jnp.float32)
    return (mixed_rows + mlp_out).astype(jnp.bfloat16)


def partners(array, axis):
    size = lax.axis_size(axis)
    return [
        lax.ppermute(array, axis, [(i, i ^ step) for i in range(size)]) for step in range(1, size)
    ]


def thirds(value):
    high = value.astype(jnp.bfloat16).astype(jnp.float32)
    rest = value - high
    middle = rest.astype(jnp.bfloat16).astype(jnp.float32)
    return high, middle, (rest - middle).astype(jnp.bfloat16).astype(jnp.float32)


def lane_ids(rows):
    return lax.broadcasted_iota(jnp.int32, (rows, LANES), 1)


def smem():
    return pl.BlockSpec(memory_space=pltpu.SMEM)


def vmem():
    return pl.BlockSpec(memory_space=pltpu.VMEM)


def stage_kernel(capacity, heads, place, lengths, rank_hbm, index_hbm, store, out_proj, up_value, *refs):
    found, pages, out_vmem, up_vmem, rank, index, table_sem, bulk_sem = refs
    tables = [
        pltpu.make_async_copy(rank_hbm, rank, table_sem.at[0]),
        pltpu.make_async_copy(index_hbm, index, table_sem.at[1]),
    ]
    share = pl.ds((place[1] % 2) * heads, heads)
    bulk = [
        pltpu.make_async_copy(store, pages, bulk_sem.at[0]),
        pltpu.make_async_copy(up_value.at[share], up_vmem, bulk_sem.at[1]),
        pltpu.make_async_copy(out_proj, out_vmem, bulk_sem.at[2]),
    ]
    for copy in tables + bulk:
        copy.start()
    for copy in tables:
        copy.wait()
    me, column = place[0], place[1]
    ranks, slots = rank.shape
    size = ranks * capacity
    for step in range(ranks):
        other = me ^ step
        length = lengths[other]
        first = step * capacity
        for k in range(capacity):
            found[first + k] = 0
            found[size + first + k] = 0
        seen = jnp.int32(0)
        for slot in range(slots):
            here = rank[other, slot] == me

            @pl.when(here)
            def _():
                start = ((column * slots + slot) % PAGES) * PAGE
                found[first + seen] = index[other, slot]
                found[size + first + seen] = jnp.clip(length - start, 0, PAGE)

            seen = seen + here.astype(jnp.int32)
    for copy in bulk:
        copy.wait()


def attend_kernel(capacity, heads, place, near_list, far_list, *refs):
    ranks = (len(refs) - 5) // 2
    query_refs, (near, far, fresh) = refs[:ranks], refs[ranks : ranks + 3]
    out_refs, (tall, held) = refs[ranks + 3 : -2], refs[-2:]
    me, column = place[0], place[1]
    rows, latent = tall.shape
    steps = rows // (ranks * heads)
    half = heads // 2
    lanes = lane_ids(rows)
    across = (((1,), (1,)), ((), ()))
    for step in range(ranks):
        rank = me ^ step
        packed = query_refs[step][...].astype(jnp.float32)
        for group in range(steps * ranks):
            for odd in range(2):
                tall[group * heads + odd * half : group * heads + (odd + 1) * half, :] = packed[
                    group * half : (group + 1) * half, odd * latent : (odd + 1) * latent
                ]
        query = tall[...].astype(jnp.bfloat16)
        scores, values = [], []
        for pages, found in ((near, near_list), (far, far_list)):
            for k in range(capacity):
                keys = pages.at[found[step * capacity + k]]
                score = jnp.dot(query, keys[...], preferred_element_type=jnp.float32) * score_scale
                live = found[(ranks + step) * capacity + k]
                scores.append(jnp.where(lanes < live, score, mask_value))
                values.append(keys)
        peak = functools.reduce(jnp.maximum, scores)
        row_peak = jnp.max(peak, axis=1, keepdims=True)
        if step == 0:
            recent = lax.dot_general(
                query, fresh[...], across, preferred_element_type=jnp.float32
            ) * score_scale
            width = recent.shape[1]
            key = lax.broadcasted_iota(jnp.int32, (rows, width), 1)
            row_step = lax.broadcasted_iota(jnp.int32, (rows, width), 0) // (ranks * heads)
            seen = (key <= row_step) & (column < 2)
            recent = jnp.where(seen, recent, mask_value)
            row_peak = jnp.maximum(row_peak, jnp.max(recent, axis=1, keepdims=True))
        total, summed = None, None
        for score, keys in zip(scores, values):
            weight = jnp.where(score > 0.5 * mask_value, jnp.exp(score - row_peak), 0.0)
            total = weight if total is None else total + weight
            part = lax.dot_general(
                weight.astype(jnp.bfloat16), keys[0:CKV, :], across, preferred_element_type=jnp.float32
            )
            summed = part if summed is None else summed + part
        row_total = jnp.sum(total, axis=1, keepdims=True)
        if step == 0:
            weight = jnp.where(seen, jnp.exp(recent - row_peak), 0.0)
            row_total = row_total + jnp.sum(weight, axis=1, keepdims=True)
            summed = summed + jnp.dot(
                weight.astype(jnp.bfloat16), fresh[:, 0:CKV], preferred_element_type=jnp.float32
            )
        extra = jnp.zeros((rows, LANES), jnp.float32)
        for lane, part in enumerate(thirds(row_peak) + thirds(row_total)):
            extra = jnp.where(lanes == lane, part, extra)
        held[:, 0:CKV] = summed
        held[:, CKV:] = extra
        for far_step, out in enumerate(out_refs):
            target = me ^ far_step
            block = [
                held[pl.ds(pl.multiple_of((u * ranks + target) * heads, heads), heads), :]
                for u in range(steps)
            ]
            start = pl.multiple_of(rank * steps * heads, steps * heads)
            out[pl.ds(start, steps * heads), :] = jnp.concatenate(block, axis=0).astype(jnp.bfloat16)


def lift_kernel(heads, ranks, *refs):
    parts, up_value, out, joined, tall = refs[:ranks], refs[ranks], refs[ranks + 1], refs[-2], refs[-1]
    count = parts[0].shape[0]
    rows = count // heads
    blocks = [part[...].astype(jnp.float32) for part in parts]
    peaks = [b[:, CKV : CKV + 1] + b[:, CKV + 1 : CKV + 2] + b[:, CKV + 2 : CKV + 3] for b in blocks]
    totals = [b[:, CKV + 3 : CKV + 4] + b[:, CKV + 4 : CKV + 5] + b[:, CKV + 5 : CKV + 6] for b in blocks]
    peak = functools.reduce(jnp.maximum, peaks)
    value, total = 0.0, 0.0
    for block, own_peak, own_total in zip(blocks, peaks, totals):
        factor = jnp.exp(own_peak - peak)
        value = value + block[:, 0:CKV] * factor
        total = total + own_total * factor
    for group in range(CKV // LANES):
        joined[group] = value[:, group * LANES : (group + 1) * LANES]
    lanes = lane_ids(count)
    tall[...] = jnp.where(lanes < 3 * heads, peak, total)
    lanes = lane_ids(rows)
    extra = jnp.zeros((rows, LANES), jnp.float32)
    for head in range(heads):
        pick = pl.ds(head % 2 * (heads // 2) + head // 2, rows, stride=heads)
        out[:, head * LANES : (head + 1) * LANES] = jnp.dot(
            jnp.concatenate([joined[g, pick, :] for g in range(CKV // LANES)], axis=1).astype(jnp.bfloat16),
            up_value[head],
            preferred_element_type=jnp.float32,
        ).astype(jnp.bfloat16)
        extra = jnp.where(lanes % heads == head, tall[pick, :], extra)
    high, middle, low = thirds(extra)
    piece = lanes // heads % 3
    out[:, heads * LANES :] = jnp.where(
        piece == 0, high, jnp.where(piece == 1, middle, low)
    ).astype(jnp.bfloat16)


def project_kernel(heads, reps, place, *refs):
    parts, (out_proj, residual, sent, kept) = refs[:reps], refs[reps:]
    core = place[1] % 2
    width = heads * LANES
    rows, steps = kept.shape[0], residual.shape[0]
    source = lax.broadcasted_iota(jnp.int32, (rows, steps), 0) - place[0] * steps
    own = source == lax.broadcasted_iota(jnp.int32, (rows, steps), 1)
    result = jnp.dot(
        own.astype(jnp.bfloat16), residual[...], preferred_element_type=jnp.float32
    )
    for side in range(2):
        blocks = [parts[step][...].astype(jnp.float32) for step in range(side, reps, 2)]
        tails = [b[:, width:] for b in blocks]

        def whole(tail, first):
            at = [pltpu.roll(tail, LANES - (first + k) * heads, 1) if first + k else tail for k in range(3)]
            return at[0] + at[1] + at[2]

        peaks = [whole(tail, 0) for tail in tails]
        totals = [whole(tail, 3) for tail in tails]
        live = lane_ids(result.shape[0]) < heads
        peaks = [jnp.where(live, p, 0.0) for p in peaks]
        totals = [jnp.where(live, t, 1.0) for t in totals]
        peak = functools.reduce(jnp.maximum, peaks)
        factors = [jnp.exp(p - peak) for p in peaks]
        total = sum(f * t for f, t in zip(factors, totals))
        factors = [f / total for f in factors]
        mixed = []
        for head in range(heads):
            lane = slice(head * LANES, (head + 1) * LANES)
            mixed.append(sum(b[:, lane] * f[:, head : head + 1] for b, f in zip(blocks, factors)))
        values = jnp.concatenate(mixed, axis=1).astype(jnp.bfloat16)
        start = pl.multiple_of((core ^ side) * width, width)
        result = result + jnp.dot(
            values, out_proj[pl.ds(start, width), :], preferred_element_type=jnp.float32
        )
    kept[...] = result
    sent[...] = result.astype(jnp.bfloat16)


def gate_kernel(ranks, *refs):
    kept, others, (gain, w_gate, w_up, out, mixed_out) = refs[0], refs[1:ranks], refs[ranks:]
    mixed = kept[...]
    for other in others:
        mixed = mixed + other[...].astype(jnp.float32)
    mixed_out[...] = mixed
    scaled = (mixed * gain[...]).astype(jnp.bfloat16)
    width = w_gate.shape[1]
    out[:, 0:width] = jnp.dot(scaled, w_gate[...], preferred_element_type=jnp.float32).astype(jnp.bfloat16)
    out[:, width : 2 * width] = jnp.dot(scaled, w_up[...], preferred_element_type=jnp.float32).astype(
        jnp.bfloat16
    )
    squares = jnp.sum(mixed * mixed, axis=1, keepdims=True)
    lanes = lane_ids(mixed.shape[0])
    extra = jnp.zeros(lanes.shape, jnp.float32)
    for lane, part in enumerate(thirds(squares)):
        extra = jnp.where(lanes == lane, part, extra)
    out[:, 2 * width :] = extra.astype(jnp.bfloat16)


def down_kernel(reps, model_width, *refs):
    parts, (w_down, out) = refs[:reps], refs[reps:]
    width = w_down.shape[0]
    total = parts[0][...].astype(jnp.float32)
    for part in parts[1:]:
        total = total + part[...].astype(jnp.float32)
    tail = total[:, 2 * width :]
    squares = jnp.sum(jnp.where(lane_ids(tail.shape[0]) < 3, tail, 0.0), axis=1, keepdims=True)
    scale = lax.rsqrt(squares / model_width + epsilon)
    gate = total[:, 0:width] * scale
    hidden = (jax.nn.silu(gate) * (total[:, width : 2 * width] * scale)).astype(jnp.bfloat16)
    out[...] = jnp.dot(hidden, w_down[...], preferred_element_type=jnp.float32).astype(jnp.bfloat16)


def call(kernel, name, operands, specs, outputs, limit, flops=0, moved=0, scratch=(), out_specs=None):
    return pl.pallas_call(
        kernel,
        name=name,
        out_shape=outputs,
        in_specs=specs,
        out_specs=jax.tree.map(lambda _: vmem(), outputs) if out_specs is None else out_specs,
        scratch_shapes=list(scratch),
        compiler_params=pltpu.CompilerParams(vmem_limit_bytes=limit),
        cost_estimate=pl.CostEstimate(flops=flops, bytes_accessed=moved, transcendentals=0),
    )(*operands)


def shape_of(shape, dtype=jnp.bfloat16):
    return jax.ShapeDtypeStruct(shape, dtype)


def queries_moved(
    latent_store,
    page_rank,
    page_index,
    lengths,
    queries,
    new_latent,
    up_value,
    out_proj,
    residual,
    norm_gain,
    w_gate,
    w_up,
    w_down,
):
    ranks, reps = lax.axis_size("dp"), lax.axis_size("rep")
    me, column = lax.axis_index("dp"), lax.axis_index("rep")
    slots = page_rank.shape[1]
    capacity = (slots + ranks - 1) // ranks
    steps, columns = residual.shape
    latent = new_latent.shape[1]
    head_count = queries.shape[1] // latent
    heads = head_count // (2 * ranks)
    rows = ranks * steps
    core_pairs = [(i, i ^ 1) for i in range(reps)]
    place = jnp.stack([me, column])

    share = lax.dynamic_index_in_dim(
        queries.reshape(steps, ranks, 2, heads * latent), column % 2, 2, keepdims=False
    ).reshape(rows * heads // 2, 2 * latent)
    arrived = [share] + partners(share, "dp")
    store = latent_store[0]
    far = lax.ppermute(store, "rep", core_pairs)
    found, near, out_near, up_near = call(
        functools.partial(stage_kernel, capacity, heads),
        "stage",
        (
            place,
            lengths.reshape(ranks),
            *[pltpu.with_memory_space_constraint(a, pltpu.HBM) for a in (page_rank, page_index, store, out_proj, up_value)],
        ),
        [smem()] * 2 + [pl.BlockSpec(memory_space=pltpu.HBM)] * 5,
        [
            shape_of((2 * ranks * capacity,), jnp.int32),
            pltpu.VMEM(store.shape, store.dtype),
            pltpu.VMEM(out_proj.shape, out_proj.dtype),
            pltpu.VMEM((heads, *up_value.shape[1:]), up_value.dtype),
        ],
        6 * MIB,
        out_specs=[smem()] + [vmem()] * 3,
        moved=2 * (store.size + out_proj.size),
        scratch=[
            pltpu.SMEM(page_rank.shape, jnp.int32),
            pltpu.SMEM(page_rank.shape, jnp.int32),
            pltpu.SemaphoreType.DMA((2,)),
            pltpu.SemaphoreType.DMA((3,)),
        ],
    )
    width = CKV + LANES
    partial_rows = call(
        functools.partial(attend_kernel, capacity, heads),
        "attend",
        (place, found, lax.ppermute(found, "rep", core_pairs), *arrived, near, far, new_latent),
        [smem()] * 3 + [vmem()] * (ranks + 3),
        [shape_of((rows * heads, width))] * ranks,
        6 * MIB,
        scratch=[
            pltpu.VMEM((rows * heads, latent), jnp.float32),
            pltpu.VMEM((rows * heads, width), jnp.float32),
        ],
        flops=2 * 2 * slots * PAGE * rows * heads * latent,
        moved=2 * near.size * 2,
    )
    joined = [partial_rows[0]] + [
        lax.ppermute(partial_rows[s], "dp", [(i, i ^ s) for i in range(ranks)]) for s in range(1, ranks)
    ]
    lifted = call(
        functools.partial(lift_kernel, heads, ranks),
        "lift",
        (*joined, up_near),
        [vmem()] * (ranks + 1),
        shape_of((rows, (heads + 1) * LANES)),
        6 * MIB,
        scratch=[
            pltpu.VMEM((CKV // LANES, rows * heads, LANES), jnp.float32),
            pltpu.VMEM((rows * heads, LANES), jnp.float32),
        ],
        flops=2 * rows * heads * CKV * LANES,
        moved=up_near.size * 2,
    )
    sent, kept = call(
        functools.partial(project_kernel, heads, reps),
        "project",
        (place, lifted, *partners(lifted, "rep"), out_near, residual),
        [smem()] + [vmem()] * (reps + 2),
        [shape_of((rows, columns)), shape_of((rows, columns), jnp.float32)],
        6 * MIB,
        flops=2 * rows * out_proj.size,
        moved=out_proj.size * 2,
    )
    gate_up, mixed = call(
        functools.partial(gate_kernel, ranks),
        "gate",
        (kept, *partners(sent, "dp"), norm_gain.reshape(1, columns), w_gate, w_up),
        [vmem()] * (ranks + 3),
        [shape_of((rows, 2 * w_gate.shape[1] + LANES)), shape_of((rows, columns), jnp.float32)],
        6 * MIB,
        flops=4 * rows * w_gate.size,
        moved=w_gate.size * 4,
    )
    down = call(
        functools.partial(down_kernel, reps, columns * reps),
        "down",
        (gate_up, *partners(gate_up, "rep"), w_down),
        [vmem()] * (reps + 1),
        shape_of((rows, columns)),
        6 * MIB,
        flops=2 * rows * w_down.size,
        moved=w_down.size * 2,
    )

    def mine(array):
        return lax.dynamic_slice_in_dim(array, me * steps, steps).astype(jnp.float32)

    return (mine(mixed) + sum(mine(a) for a in [down] + partners(down, "dp"))).astype(jnp.bfloat16)


def on_device(*arrays):
    ranks = lax.axis_size("dp")
    lengths, queries, new_latent = arrays[3:6]
    heads = queries.shape[1] // new_latent.shape[1]
    if ranks <= 8 and heads % (16 * ranks) == 0 and lengths.shape[1] == 1:
        return queries_moved(*arrays)
    return pages_moved(*arrays)


def solution(mesh):
    in_specs = (
        P(("groups", "dp"), "rep", None, None),
        P("groups", "rep"),
        P("groups", "rep"),
        P("groups", None),
        P(("groups", "dp"), None),
        P(("groups", "dp"), None),
        P("dp", None, None),
        P("dp", "rep"),
        P(("groups", "dp"), "rep"),
        P("rep"),
        P("rep", "dp"),
        P("rep", "dp"),
        P("dp", "rep"),
    )
    out_specs = P(("groups", "dp"), "rep")
    return jax.shard_map(
        on_device, mesh=mesh, in_specs=in_specs, out_specs=out_specs, check_vma=False
    )
```

```python
import functools
import math

import jax
import jax.numpy as jnp
from jax import lax
from jax.experimental import pallas as pl
from jax.experimental.pallas import tpu as pltpu
from jax.sharding import PartitionSpec as P


CKV = 512
PAGE = 128
PAGES = 48
LANES = 128
MIB = 1 << 20

score_scale = 1.0 / math.sqrt(192.0)
epsilon = 1e-06
mask_value = -1e30


def merged_2(array, axis, join):
    gathered = jax.tree.map(
        lambda a, kind: lax.all_gather(a.astype(kind), axis),
        array,
        jax.tree.map(lambda a: jnp.bfloat16 if a.dtype == jnp.float32 else a.dtype, array),
    )

    def take(source):
        return jax.tree.map(
            lambda a, own: lax.dynamic_index_in_dim(a, source, 0, False).astype(own.dtype),
            gathered,
            array,
        )

    return lax.fori_loop(
        1, lax.axis_size(axis), lambda source, state: join(state, take(source)), take(0)
    )


def page_partials(page_keys, page_queries, key_counts):
    scores = (
        jnp.einsum("pshl,plt->psht", page_queries, page_keys, preferred_element_type=jnp.float32)
        * score_scale
    )
    places = lax.broadcasted_iota(jnp.int32, scores.shape, 3)
    visible = places < key_counts[:, None, None, None]
    scores = jnp.where(visible, scores, mask_value)
    row_peak = jnp.max(scores, axis=3)
    weights = jnp.where(visible, jnp.exp(scores - row_peak[..., None]), 0.0)
    row_total = jnp.sum(weights, axis=3)
    partial_value = jnp.einsum(
        "psht,pct->pshc",
        weights.astype(jnp.bfloat16),
        page_keys[:, :CKV, :],
        preferred_element_type=jnp.float32,
    )
    return (partial_value, row_peak, row_total)


def join_pages(partial_value, row_peak, row_total, slot_request, requests):
    owner_mask = slot_request[None, :] == jnp.arange(requests, dtype=jnp.int32)[:, None]
    spread = owner_mask[:, :, None, None]
    best_peak = jnp.max(jnp.where(spread, row_peak[None], mask_value), axis=1)
    factor = jnp.where(spread, jnp.exp(row_peak[None] - best_peak[:, None]), 0.0)
    joined = jnp.einsum("jpsh,pshc->jshc", factor, partial_value, precision=lax.Precision.HIGHEST)
    summed = jnp.sum(factor * row_total[None], axis=1)
    return (joined, best_peak, summed)


def combine(former, latter):
    former_sum, former_peak, former_total = former
    latter_sum, latter_peak, latter_total = latter
    highest = jnp.maximum(former_peak, latter_peak)
    former_scale = jnp.exp(former_peak - highest)
    latter_scale = jnp.exp(latter_peak - highest)
    merged_sum = former_sum * former_scale[..., None] + latter_sum * latter_scale[..., None]
    return (merged_sum, highest, former_total * former_scale + latter_total * latter_scale)


def fresh_partial(query_rows, fresh_rows, active):
    scores = (
        jnp.einsum("jshl,jul->jshu", query_rows, fresh_rows, preferred_element_type=jnp.float32)
        * score_scale
    )
    step_query = lax.broadcasted_iota(jnp.int32, scores.shape, 1)
    step_key = lax.broadcasted_iota(jnp.int32, scores.shape, 3)
    visible = (step_key <= step_query) & active
    scores = jnp.where(visible, scores, mask_value)
    row_peak = jnp.max(scores, axis=3)
    weights = jnp.where(visible, jnp.exp(scores - row_peak[..., None]), 0.0)
    row_total = jnp.sum(weights, axis=3)
    partial_value = jnp.einsum(
        "jshu,juc->jshc",
        weights.astype(jnp.bfloat16),
        fresh_rows[:, :, :CKV],
        preferred_element_type=jnp.float32,
    )
    return (partial_value, row_peak, row_total)


def pages_moved(
    latent_store,
    page_rank,
    page_index,
    lengths,
    queries,
    new_latent,
    up_value,
    out_proj,
    residual,
    norm_gain,
    w_gate,
    w_up,
    w_down,
):
    my_rank = lax.axis_index("dp")
    my_column = lax.axis_index("rep")
    rank_count, slot_count = page_rank.shape
    capacity = (slot_count + rank_count - 1) // rank_count
    requests = lengths.shape[1]
    rows_here = residual.shape[0]
    steps_count = rows_here // requests
    latent_width = new_latent.shape[1]
    head_count = queries.shape[1] // latent_width
    query_rows = queries.reshape(requests, steps_count, head_count, latent_width)
    fresh_rows = new_latent.reshape(requests, steps_count, latent_width)
    slot_order = jnp.arange(slot_count, dtype=jnp.int32)
    request_ids = jnp.arange(requests, dtype=jnp.int32)
    cap_ids = jnp.arange(capacity, dtype=jnp.int32)
    global_slot = my_column * slot_count + slot_order
    slot_request = global_slot // PAGES
    slot_page = global_slot % PAGES
    own_lengths = lax.dynamic_index_in_dim(lengths, my_rank, 0, keepdims=False)
    slot_length = jnp.sum(
        jnp.where(slot_request[:, None] == request_ids[None, :], own_lengths[None, :], 0), axis=1
    )
    key_counts = jnp.clip(slot_length - slot_page * PAGE, 0, PAGE)
    my_sources = lax.dynamic_index_in_dim(page_rank, my_rank, 0, keepdims=False)
    earlier = (my_sources[None, :] == my_sources[:, None]) & (
        slot_order[None, :] < slot_order[:, None]
    )
    arrival_rank = jnp.sum(earlier.astype(jnp.int32), axis=1)
    arrival_slot = my_sources * capacity + arrival_rank
    held_here = page_rank == my_rank
    held_order = jnp.cumsum(held_here.astype(jnp.int32), axis=1) - 1
    selector = held_here[:, None, :] & (held_order[:, None, :] == cap_ids[None, :, None])
    sent_valid = jnp.any(selector, axis=2).reshape(-1)
    sent_page = jnp.sum(jnp.where(selector, page_index[:, None, :], 0), axis=2).reshape(-1)
    stored = latent_store[0]
    outgoing = jnp.take(stored, sent_page, axis=0)
    outgoing = jnp.where(sent_valid[:, None, None], outgoing, jnp.zeros_like(outgoing))
    arrived = lax.all_to_all(outgoing, "dp", split_axis=0, concat_axis=0, tiled=True)
    restored = jnp.take(arrived, arrival_slot, axis=0)
    page_queries = jnp.take(query_rows, slot_request, axis=0)
    partial_value, row_peak, row_total = page_partials(restored, page_queries, key_counts)
    joined = join_pages(partial_value, row_peak, row_total, slot_request, requests)
    local_part = combine(joined, fresh_partial(query_rows, fresh_rows, my_column == 0))
    merged = merged_2(local_part, "rep", combine)
    attention = (
        (merged[0] / merged[2][..., None]).astype(jnp.bfloat16).reshape(rows_here, head_count, CKV)
    )
    headed = lax.all_to_all(attention, "dp", split_axis=1, concat_axis=0, tiled=True)
    values = jnp.einsum("rhc,hcv->rhv", headed, up_value, preferred_element_type=jnp.float32)
    values = values.astype(jnp.bfloat16).reshape(headed.shape[0], -1)
    picked = values
    attn_out = lax.psum_scatter(
        jnp.dot(picked, out_proj, preferred_element_type=jnp.float32).astype(jnp.bfloat16),
        "dp",
        scatter_dimension=0,
        tiled=True,
    ).astype(jnp.float32)
    mixed_rows = residual.astype(jnp.float32) + attn_out
    squares = lax.psum(jnp.sum(mixed_rows * mixed_rows, axis=1), "rep")
    normed = (mixed_rows * lax.rsqrt(squares / (norm_gain.shape[0] * lax.axis_size("rep")) + epsilon)[:, None] * norm_gain).astype(
        jnp.bfloat16
    )
    piece = lax.all_gather(normed, "dp", axis=0, tiled=True)
    gate_part = jnp.dot(piece, w_gate, preferred_element_type=jnp.float32)
    up_part = jnp.dot(piece, w_up, preferred_element_type=jnp.float32)
    partial_rows = jnp.concatenate([gate_part, up_part], axis=1)
    gate_up = lax.psum(partial_rows.astype(jnp.bfloat16), "rep").astype(jnp.float32)
    hidden_width = w_gate.shape[1]
    hidden = (jax.nn.silu(gate_up[:, :hidden_width]) * gate_up[:, hidden_width:]).astype(
        jnp.bfloat16
    )
    picked = hidden
    mlp_out = lax.psum_scatter(
        jnp.dot(picked, w_down, preferred_element_type=jnp.float32).astype(jnp.bfloat16),
        "dp",
        scatter_dimension=0,
        tiled=True,
    ).astype(jnp.float32)
    return (mixed_rows + mlp_out).astype(jnp.bfloat16)


def hops(size, name):
    order = list(range(1, size))
    if name in ("query", "partial"):
        return [order[0], *reversed(order[1:])]
    if name == "units":
        return [order[-1], *order[:-1]]
    return order


def partners(arrays, axis, name):
    size = lax.axis_size(axis)
    moved = {}
    for step in hops(size, name):
        moved[step] = lax.ppermute(arrays[step], axis, [(i, i ^ step) for i in range(size)])
    return [moved[step] for step in range(1, size)]


def thirds(value):
    high = value.astype(jnp.bfloat16).astype(jnp.float32)
    rest = value - high
    middle = rest.astype(jnp.bfloat16).astype(jnp.float32)
    return high, middle, (rest - middle).astype(jnp.bfloat16).astype(jnp.float32)


def lane_ids(rows):
    return lax.broadcasted_iota(jnp.int32, (rows, LANES), 1)


def smem():
    return pl.BlockSpec(memory_space=pltpu.SMEM)


def vmem():
    return pl.BlockSpec(memory_space=pltpu.VMEM)


def position():
    return lax.axis_index("dp"), lax.axis_index("rep")


def pack_kernel(queries, out, held, rows, sem):
    _, column = position()
    ranks, steps, width = held.shape
    pairs = rows.shape[0] // (ranks * steps)
    double = rows.shape[1]
    copies = []
    for rank in range(ranks):
        start = pl.multiple_of((2 * rank + column % 2) * width, LANES)
        copies.append(
            pltpu.make_async_copy(queries.at[:, pl.ds(start, width)], held.at[rank], sem.at[rank])
        )
        copies[-1].start()
    for rank, copy in enumerate(copies):
        copy.wait()
        part = held[rank].astype(jnp.float32)
        for step in range(steps):
            for pair in range(pairs):
                row = (rank * steps + step) * pairs + pair
                rows[row : row + 1, :] = part[step : step + 1, pair * double : (pair + 1) * double]
    out[...] = rows[...].astype(jnp.bfloat16)


def stage_kernel(capacity, heads, lengths_hbm, rank_hbm, index_hbm, store, up_value, new_latent, *refs):
    found, pages, up_vmem, fresh, lengths, rank, index, table_sem, bulk_sem = refs
    me, column = position()
    tables = [
        pltpu.make_async_copy(source, target, table_sem.at[k])
        for k, (source, target) in enumerate(
            ((lengths_hbm, lengths), (rank_hbm, rank), (index_hbm, index))
        )
    ]
    share = pl.ds((column % 2) * heads, heads)
    bulk = [
        pltpu.make_async_copy(store, pages, bulk_sem.at[0]),
        pltpu.make_async_copy(up_value.at[share], up_vmem, bulk_sem.at[1]),
        pltpu.make_async_copy(new_latent, fresh, bulk_sem.at[2]),
    ]
    for copy in tables + bulk:
        copy.start()
    for copy in tables:
        copy.wait()
    ranks, slots = rank.shape
    size = ranks * capacity
    for step in range(ranks):
        other = me ^ step
        length = lengths[other]
        first = step * capacity
        for k in range(capacity):
            found[first + k] = 0
            found[size + first + k] = 0
        seen = jnp.int32(0)
        for slot in range(slots):
            here = rank[other, slot] == me

            @pl.when(here)
            def _():
                start = ((column * slots + slot) % PAGES) * PAGE
                found[first + seen] = index[other, slot]
                found[size + first + seen] = jnp.clip(length - start, 0, PAGE)

            seen = seen + here.astype(jnp.int32)
    for copy in bulk:
        copy.wait()


def attend_kernel(capacity, heads, near_list, far_list, *refs):
    ranks = (len(refs) - 7) // 2
    query_refs, (near, far, fresh, out_proj) = refs[:ranks], refs[ranks : ranks + 4]
    out_refs, (out_near, held, sem) = refs[ranks + 4 : -3], refs[-3:]
    fetch = pltpu.make_async_copy(out_proj, out_near, sem)
    fetch.start()
    me, column = position()
    rows = held.shape[1]
    latent = fresh.shape[1]
    steps = rows // (ranks * heads)
    half = heads // 2
    lanes = lane_ids(rows)
    across = (((1,), (1,)), ((), ()))
    for step in range(ranks):
        packed = query_refs[step][...]
        query = jnp.concatenate([packed[:, 0:latent], packed[:, latent:]], axis=0)
        scores, keys = [], []
        for k in range(capacity):
            pages, live = [], []
            for side, table in ((near, near_list), (far, far_list)):
                pages.append(side[table[step * capacity + k]])
                live.append(lanes < table[(ranks + step) * capacity + k])
            keys.append(jnp.concatenate(pages, axis=1))
            score = jnp.dot(query, keys[-1], preferred_element_type=jnp.float32) * score_scale
            scores.append(jnp.where(jnp.concatenate(live, axis=1), score, mask_value))
        row_peak = jnp.max(functools.reduce(jnp.maximum, scores), axis=1, keepdims=True)
        if step == 0:
            recent = lax.dot_general(
                query, fresh[...], across, preferred_element_type=jnp.float32
            ) * score_scale
            width = recent.shape[1]
            key = lax.broadcasted_iota(jnp.int32, (rows, width), 1)
            row_step = lax.broadcasted_iota(jnp.int32, (rows, width), 0) // half % steps
            seen = (key <= row_step) & (column < 2)
            recent = jnp.where(seen, recent, mask_value)
            row_peak = jnp.maximum(row_peak, jnp.max(recent, axis=1, keepdims=True))
        total, summed = None, None
        for score, key_block in zip(scores, keys):
            weight = jnp.where(score > 0.5 * mask_value, jnp.exp(score - row_peak), 0.0)
            total = weight if total is None else total + weight
            part = lax.dot_general(
                weight.astype(jnp.bfloat16), key_block[0:CKV, :], across, preferred_element_type=jnp.float32
            )
            summed = part if summed is None else summed + part
        row_total = jnp.sum(total, axis=1, keepdims=True)
        if step == 0:
            weight = jnp.where(seen, jnp.exp(recent - row_peak), 0.0)
            row_total = row_total + jnp.sum(weight, axis=1, keepdims=True)
            summed = summed + jnp.dot(
                weight.astype(jnp.bfloat16), fresh[:, 0:CKV], preferred_element_type=jnp.float32
            )
        extra = jnp.zeros((rows, LANES), jnp.float32)
        for lane, part in enumerate(thirds(row_peak) + thirds(row_total)):
            extra = jnp.where(lanes == lane, part, extra)
        held[step, :, 0:CKV] = summed
        held[step, :, CKV:] = extra
    count = steps * half
    for step in range(ranks):
        start = pl.multiple_of((me ^ step) * 2 * count, 2 * count)
        for far_step, out in enumerate(out_refs):
            target = me ^ far_step
            block = [
                held[step, pl.ds(pl.multiple_of((odd * ranks + target) * count, count), count), :]
                for odd in range(2)
            ]
            out[pl.ds(start, 2 * count), :] = jnp.concatenate(block, axis=0).astype(jnp.bfloat16)
    fetch.wait()


def lift_kernel(heads, ranks, *refs):
    parts, up_value, out, joined, tall = refs[:ranks], refs[ranks], refs[ranks + 1], refs[-2], refs[-1]
    count = parts[0].shape[0]
    rows = count // heads
    steps, half = rows // ranks, heads // 2
    blocks = [part[...].astype(jnp.float32) for part in parts]
    peaks = [b[:, CKV : CKV + 1] + b[:, CKV + 1 : CKV + 2] + b[:, CKV + 2 : CKV + 3] for b in blocks]
    totals = [b[:, CKV + 3 : CKV + 4] + b[:, CKV + 4 : CKV + 5] + b[:, CKV + 5 : CKV + 6] for b in blocks]
    peak = functools.reduce(jnp.maximum, peaks)
    value, total = 0.0, 0.0
    for block, own_peak, own_total in zip(blocks, peaks, totals):
        factor = jnp.exp(own_peak - peak)
        value = value + block[:, 0:CKV] * factor
        total = total + own_total * factor
    for group in range(CKV // LANES):
        joined[group] = value[:, group * LANES : (group + 1) * LANES]
    lanes = lane_ids(count)
    tall[...] = jnp.where(lanes < 3 * heads, peak, total)
    lanes = lane_ids(rows)
    extra = jnp.zeros((rows, LANES), jnp.float32)

    def rows_of(read, head):
        first = (head % 2) * steps * half + head // 2
        return jnp.concatenate(
            [read(pl.ds(first + step * half, ranks, stride=steps * heads)) for step in range(steps)], axis=0
        )

    for head in range(heads):
        value = jnp.concatenate(
            [rows_of(lambda at: joined[g, at, :], head) for g in range(CKV // LANES)], axis=1
        )
        out[:, head * LANES : (head + 1) * LANES] = jnp.dot(
            value.astype(jnp.bfloat16), up_value[head], preferred_element_type=jnp.float32
        ).astype(jnp.bfloat16)
        extra = jnp.where(lanes % heads == head, rows_of(lambda at: tall[at, :], head), extra)
    high, middle, low = thirds(extra)
    piece = lanes // heads % 3
    out[:, heads * LANES :] = jnp.where(
        piece == 0, high, jnp.where(piece == 1, middle, low)
    ).astype(jnp.bfloat16)


def project_kernel(heads, reps, ranks, *refs):
    parts, (out_proj, residual, sent, kept) = refs[:reps], refs[reps:]
    me, column = position()
    width = heads * LANES
    rows, steps = kept.shape[0], residual.shape[0]
    row = lax.broadcasted_iota(jnp.int32, (rows, steps), 0)
    own = row == lax.broadcasted_iota(jnp.int32, (rows, steps), 1) * ranks + me
    result = jnp.dot(
        own.astype(jnp.bfloat16), residual[...], preferred_element_type=jnp.float32
    )
    for side in range(2):
        blocks = [parts[step][...].astype(jnp.float32) for step in range(side, reps, 2)]
        tails = [b[:, width:] for b in blocks]

        def whole(tail, first):
            at = [pltpu.roll(tail, LANES - (first + k) * heads, 1) if first + k else tail for k in range(3)]
            return at[0] + at[1] + at[2]

        peaks = [whole(tail, 0) for tail in tails]
        totals = [whole(tail, 3) for tail in tails]
        live = lane_ids(rows) < heads
        peaks = [jnp.where(live, p, 0.0) for p in peaks]
        totals = [jnp.where(live, t, 1.0) for t in totals]
        peak = functools.reduce(jnp.maximum, peaks)
        factors = [jnp.exp(p - peak) for p in peaks]
        total = sum(f * t for f, t in zip(factors, totals))
        factors = [f / total for f in factors]
        mixed = []
        for head in range(heads):
            lane = slice(head * LANES, (head + 1) * LANES)
            mixed.append(sum(b[:, lane] * f[:, head : head + 1] for b, f in zip(blocks, factors)))
        values = jnp.concatenate(mixed, axis=1).astype(jnp.bfloat16)
        start = pl.multiple_of((column % 2 ^ side) * width, width)
        result = result + jnp.dot(
            values, out_proj[pl.ds(start, width), :], preferred_element_type=jnp.float32
        )
    kept[...] = result
    sent[...] = result.astype(jnp.bfloat16)


def gate_kernel(ranks, *refs):
    kept, others, (gain, w_gate, w_up, out, mixed_out) = refs[0], refs[1:ranks], refs[ranks:]
    mixed = kept[...]
    for other in others:
        mixed = mixed + other[...].astype(jnp.float32)
    mixed_out[...] = mixed
    scaled = (mixed * gain[...]).astype(jnp.bfloat16)
    width = w_gate.shape[1]
    out[:, 0:width] = jnp.dot(scaled, w_gate[...], preferred_element_type=jnp.float32).astype(jnp.bfloat16)
    out[:, width : 2 * width] = jnp.dot(scaled, w_up[...], preferred_element_type=jnp.float32).astype(
        jnp.bfloat16
    )
    squares = jnp.sum(mixed * mixed, axis=1, keepdims=True)
    lanes = lane_ids(mixed.shape[0])
    extra = jnp.zeros(lanes.shape, jnp.float32)
    for lane, part in enumerate(thirds(squares)):
        extra = jnp.where(lanes == lane, part, extra)
    out[:, 2 * width :] = extra.astype(jnp.bfloat16)


def down_kernel(reps, model_width, *refs):
    parts, (w_down, out) = refs[:reps], refs[reps:]
    width = w_down.shape[0]
    total = parts[0][...].astype(jnp.float32)
    for part in parts[1:]:
        total = total + part[...].astype(jnp.float32)
    tail = total[:, 2 * width :]
    squares = jnp.sum(jnp.where(lane_ids(tail.shape[0]) < 3, tail, 0.0), axis=1, keepdims=True)
    scale = lax.rsqrt(squares / model_width + epsilon)
    gate = total[:, 0:width] * scale
    hidden = (jax.nn.silu(gate) * (total[:, width : 2 * width] * scale)).astype(jnp.bfloat16)
    out[...] = jnp.dot(hidden, w_down[...], preferred_element_type=jnp.float32).astype(jnp.bfloat16)


def finish_kernel(ranks, mixed, *refs):
    parts, out = refs[:ranks], refs[ranks]
    me, _ = position()
    total = mixed[...]
    for part in parts:
        total = total + part[...].astype(jnp.float32)
    row = lax.broadcasted_iota(jnp.int32, total.shape, 0)
    picked = [
        jnp.sum(jnp.where(row == step * ranks + me, total, 0.0), axis=0, keepdims=True)
        for step in range(out.shape[0])
    ]
    out[...] = jnp.concatenate(picked, axis=0).astype(jnp.bfloat16)


def call(kernel, operands, specs, outputs, flops=0, moved=0, scratch=(), out_specs=None):
    return pl.pallas_call(
        kernel,
        out_shape=outputs,
        in_specs=specs,
        out_specs=jax.tree.map(lambda _: vmem(), outputs) if out_specs is None else out_specs,
        scratch_shapes=list(scratch),
        compiler_params=pltpu.CompilerParams(vmem_limit_bytes=6 * MIB),
        cost_estimate=pl.CostEstimate(flops=flops, bytes_accessed=moved, transcendentals=0),
    )(*operands)


def in_hbm(*arrays):
    return [pltpu.with_memory_space_constraint(a, pltpu.HBM) for a in arrays]


def hbm():
    return pl.BlockSpec(memory_space=pltpu.HBM)


def shape_of(shape, dtype=jnp.bfloat16):
    return jax.ShapeDtypeStruct(shape, dtype)


def queries_moved(
    latent_store,
    page_rank,
    page_index,
    lengths,
    queries,
    new_latent,
    up_value,
    out_proj,
    residual,
    norm_gain,
    w_gate,
    w_up,
    w_down,
):
    ranks, reps = lax.axis_size("dp"), lax.axis_size("rep")
    slots = page_rank.shape[1]
    capacity = (slots + ranks - 1) // ranks
    steps, columns = residual.shape
    latent = new_latent.shape[1]
    head_count = queries.shape[1] // latent
    heads = head_count // (2 * ranks)
    rows = ranks * steps
    core_pairs = [(i, i ^ 1) for i in range(reps)]

    packed_shape = (rows * heads // 2, 2 * latent)
    share = call(
        pack_kernel,
        in_hbm(queries),
        [hbm()],
        shape_of(packed_shape),
        moved=queries.size * 2,
        scratch=[
            pltpu.VMEM((ranks, steps, heads * latent), jnp.bfloat16),
            pltpu.VMEM(packed_shape, jnp.float32),
            pltpu.SemaphoreType.DMA((ranks,)),
        ],
    )
    arrived = [share] + partners([share] * ranks, "dp", "query")
    store = latent_store[0]
    far = lax.ppermute(store, "rep", core_pairs)
    found, near, up_near, fresh = call(
        functools.partial(stage_kernel, capacity, heads),
        in_hbm(lengths.reshape(ranks), page_rank, page_index, store, up_value, new_latent),
        [hbm()] * 6,
        [
            shape_of((2 * ranks * capacity,), jnp.int32),
            pltpu.VMEM(store.shape, store.dtype),
            pltpu.VMEM((heads, *up_value.shape[1:]), up_value.dtype),
            pltpu.VMEM(new_latent.shape, new_latent.dtype),
        ],
        out_specs=[smem()] + [vmem()] * 3,
        moved=2 * store.size,
        scratch=[
            pltpu.SMEM((ranks,), jnp.int32),
            pltpu.SMEM(page_rank.shape, jnp.int32),
            pltpu.SMEM(page_rank.shape, jnp.int32),
            pltpu.SemaphoreType.DMA((3,)),
            pltpu.SemaphoreType.DMA((3,)),
        ],
    )
    width = CKV + LANES
    *partial_rows, out_near = call(
        functools.partial(attend_kernel, capacity, heads),
        (found, lax.ppermute(found, "rep", core_pairs), *arrived, near, far, fresh, *in_hbm(out_proj)),
        [smem()] * 2 + [vmem()] * (ranks + 3) + [hbm()],
        [shape_of((rows * heads, width))] * ranks + [pltpu.VMEM(out_proj.shape, out_proj.dtype)],
        out_specs=[vmem()] * (ranks + 1),
        scratch=[
            pltpu.VMEM((ranks, rows * heads, width), jnp.float32),
            pltpu.SemaphoreType.DMA,
        ],
        flops=2 * 2 * slots * PAGE * rows * heads * latent,
        moved=2 * store.size * 2 + 2 * out_proj.size,
    )
    lifted = call(
        functools.partial(lift_kernel, heads, ranks),
        (partial_rows[0], *partners(partial_rows, "dp", "partial"), up_near),
        [vmem()] * (ranks + 1),
        shape_of((rows, (heads + 1) * LANES)),
        scratch=[
            pltpu.VMEM((CKV // LANES, rows * heads, LANES), jnp.float32),
            pltpu.VMEM((rows * heads, LANES), jnp.float32),
        ],
        flops=2 * rows * heads * CKV * LANES,
        moved=up_near.size * 2,
    )
    sent, kept = call(
        functools.partial(project_kernel, heads, reps, ranks),
        (lifted, *partners([lifted] * reps, "rep", "lifted"), out_near, residual),
        [vmem()] * (reps + 2),
        [shape_of((rows, columns)), shape_of((rows, columns), jnp.float32)],
        flops=2 * rows * out_proj.size,
        moved=out_proj.size * 2,
    )
    gate_up, mixed = call(
        functools.partial(gate_kernel, ranks),
        (kept, *partners([sent] * ranks, "dp", "mixed"), norm_gain.reshape(1, columns), w_gate, w_up),
        [vmem()] * (ranks + 3),
        [shape_of((rows, 2 * w_gate.shape[1] + LANES)), shape_of((rows, columns), jnp.float32)],
        flops=4 * rows * w_gate.size,
        moved=w_gate.size * 4,
    )
    down = call(
        functools.partial(down_kernel, reps, columns * reps),
        (gate_up, *partners([gate_up] * reps, "rep", "units"), w_down),
        [vmem()] * (reps + 1),
        shape_of((rows, columns)),
        flops=2 * rows * w_down.size,
        moved=w_down.size * 2,
    )
    return call(
        functools.partial(finish_kernel, ranks),
        (mixed, down, *partners([down] * ranks, "dp", "down")),
        [vmem()] * (ranks + 1),
        shape_of((steps, columns)),
        moved=rows * columns * 12,
    )


def share_of_latent_work(mesh):
    return mesh.shape["dp"] <= 8 and mesh.shape["rep"] % 2 == 0


def on_device(*arrays):
    lengths, queries, new_latent = arrays[3:6]
    heads = queries.shape[1] // new_latent.shape[1]
    if heads % (16 * lax.axis_size("dp")) or lengths.shape[1] != 1:
        raise ValueError("unsupported shapes")
    return queries_moved(*arrays)


def solution(mesh):
    in_specs = (
        P(("groups", "dp"), "rep", None, None),
        P("groups", "rep"),
        P("groups", "rep"),
        P("groups", None),
        P(("groups", "dp"), None),
        P(("groups", "dp"), None),
        P("dp", None, None),
        P("dp", "rep"),
        P(("groups", "dp"), "rep"),
        P("rep"),
        P("rep", "dp"),
        P("rep", "dp"),
        P("dp", "rep"),
    )
    out_specs = P(("groups", "dp"), "rep")
    moves = share_of_latent_work(mesh)
    return jax.shard_map(
        on_device if moves else pages_moved,
        mesh=mesh,
        in_specs=in_specs,
        out_specs=out_specs,
        check_vma=False,
    )
```
